256 devices in a mesh: harm: 8 (over x, y_lo), dom: 32 (over y_hi, z, core).
Axes of the slice: x: 4, y: 4 (y_hi: 2, y_lo: 2; y = y_hi * 2 + y_lo), z: 8, core: 2. Of those that a mesh axis runs over, the one named last changes fastest.
Arguments:
- response: float32 [2, 64, 64, 8192], P(None, 'harm', None, 'dom'), may hold values from -6 to 6
- base_coeff: float32 [2, 17, 64, 8192], P(None, None, None, 'dom'), may hold values from -1.5 to 1.5
- volume_mat: float32 [64, 64], replicated, may hold values from -0.75 to 0.75
- trace_mats: float32 [4, 16, 64], replicated, may hold values from -0.75 to 0.75
- lift_mat: float32 [64, 16], replicated, may hold values from -1.5 to 1.5
- round_masks: int32 [4], replicated, may hold values from 1 to 31, as said below
- send_elem: int32 [4, 2048], P(None, 'dom'), may hold values from 0 to 255
- send_face: int32 [4, 2048], P(None, 'dom'), may hold values from 0 to 3
- recv_elem: int32 [4, 2048], P(None, 'dom'), may hold values from 0 to 255
Outputs:
- image: float32 [2, 64, 64, 8192], P(None, 'harm', None, 'dom')
The draws below stay inside these ranges and needn't reach their ends.
Inputs may be any that keep to these rules, and one draw needn't show every extreme that they name: `round_masks`: 4 distinct masks, among them the smallest and the largest possible mask; in each round partition p is matched with partition p XOR mask.
All inputs are finite; a program needn't handle non-finite values.
Results may differ from the reference program's by a relative error of at most 0.0001.
Values sent between devices are 32-bit elements; how exact they have to be, the bound alone decides.
No kernel may reach another device: no remote copies, remote signals or barrier semaphores. Data moves between devices by JAX's collectives and lax.ppermute only.
A program may use at most 64 MiB of HBM per device.

```python
import jax
import jax.numpy as jnp
from jax import lax

NH = 64
REACH = 8
NODE_VARS = 64
FACE_VARS = 16
ROUNDS = 4
E_LOC = 256
FACES = 64
E_TOTAL = 8192
SLOTS = 2048
N_DOM = 32


def draw_round_masks(key, part):
    middle = jax.random.permutation(jax.random.fold_in(key, 11), N_DOM - 3) + 2
    masks = jnp.concatenate([jnp.array([1, N_DOM - 1], jnp.int32), middle[:ROUNDS - 2].astype(jnp.int32)])
    order = jax.random.permutation(jax.random.fold_in(key, 13), ROUNDS)
    return masks[order].astype(jnp.int32)


def place_ends(drawn, key, least, top_value):
    longest = drawn.shape.index(max(drawn.shape))
    spots = []
    for shift in (0, 1):
        where = [jax.random.randint(jax.random.fold_in(key, axis), (), 0, length) for axis, length in enumerate(drawn.shape)]
        where[longest] = (where[longest] + shift) % drawn.shape[longest]
        spots.append(tuple(where))
    return drawn.at[spots[0]].set(least).at[spots[1]].set(top_value)


def block_levels(rng, dims, shards, least, top_value):
    gain, own = 1.0, jax.random.fold_in(rng, 6)
    for position, parts in shards:
        heights = jnp.exp(jax.random.uniform(jax.random.fold_in(own, position), (parts,), jnp.float32, least / len(shards), top_value / len(shards)))
        gain = gain * jnp.repeat(heights, dims[position] // parts).reshape([-1 if axis == position else 1 for axis in range(len(dims))])
    return gain


def scatter_about(own_key, dims, width, most, cuts=(), held_as=jnp.bfloat16):
    drawn = width * jax.random.normal(own_key, dims, jnp.float32)
    if cuts:
        drawn = drawn * block_levels(own_key, dims, cuts, -0.22, 0.18)
    return jnp.clip(drawn, -most, most).astype(held_as)


def setup_inputs(seed: int = 0) -> dict:
    arg_keys = jax.random.split(jax.random.key(seed), 10)
    return {
        "response": scatter_about(arg_keys[0], (2, NH, NODE_VARS, E_TOTAL), 1.0, 6.0, ((1, 8), (3, 32)), jnp.float32),
        "base_coeff": scatter_about(arg_keys[1], (2, 2 * REACH + 1, NODE_VARS, E_TOTAL), 0.25, 1.5, ((3, 32),), jnp.float32),
        "volume_mat": scatter_about(arg_keys[2], (NODE_VARS, NODE_VARS), NODE_VARS ** -0.5, 0.75, (), jnp.float32),
        "trace_mats": scatter_about(arg_keys[3], (4, FACE_VARS, NODE_VARS), NODE_VARS ** -0.5, 0.75, (), jnp.float32),
        "lift_mat": scatter_about(arg_keys[4], (NODE_VARS, FACE_VARS), FACE_VARS ** -0.5, 1.5, (), jnp.float32),
        "round_masks": draw_round_masks(jax.random.fold_in(arg_keys[9], 71), 0),
        "send_elem": place_ends(jax.random.randint(arg_keys[6], (ROUNDS, SLOTS), 0, E_LOC), jax.random.fold_in(arg_keys[6], 1), 0, E_LOC - 1).astype(jnp.int32),
        "send_face": place_ends(jax.random.randint(arg_keys[7], (ROUNDS, SLOTS), 0, 4), jax.random.fold_in(arg_keys[7], 1), 0, 3).astype(jnp.int32),
        "recv_elem": place_ends(jax.random.randint(arg_keys[8], (ROUNDS, SLOTS), 0, E_LOC), jax.random.fold_in(arg_keys[8], 1), 0, E_LOC - 1).astype(jnp.int32),
    }


base_omega = 0.2


def convolve(field, coeff):
    real_acc = jnp.zeros(field.shape[1:], jnp.float32)
    imag_acc = jnp.zeros(field.shape[1:], jnp.float32)
    for offset in range(-REACH, REACH + 1):
        shifted = jnp.roll(field, offset, axis=1)
        c_real = coeff[0, offset + REACH][None]
        c_imag = coeff[1, offset + REACH][None]
        real_acc = real_acc + c_real * shifted[0] - c_imag * shifted[1]
        imag_acc = imag_acc + c_real * shifted[1] + c_imag * shifted[0]
    return jnp.stack([real_acc, imag_acc])


def face_select(trace_mats, faces):
    select = jnp.zeros(faces.shape + trace_mats.shape[1:], jnp.float32)
    for face_id in range(4):
        select = select + jnp.where((faces == face_id)[..., None, None], trace_mats[face_id], 0.0)
    return select


def reference(response, base_coeff, volume_mat, trace_mats, lift_mat, round_masks, send_elem, send_face, recv_elem):
    conv = convolve(response, base_coeff)
    slot_ids = jnp.arange(NH, dtype=jnp.int32)
    wave_number = jnp.where(slot_ids < NH // 2, slot_ids, slot_ids - NH).astype(jnp.float32)
    frequency = base_omega * wave_number[:, None, None]
    derived = jnp.einsum('ab,cjbe->cjae', volume_mat, conv, precision=lax.Precision.HIGHEST)
    image = jnp.stack([derived[0] - frequency * response[1], derived[1] + frequency * response[0]])
    home = jnp.arange(N_DOM, dtype=jnp.int32)
    for step_round in range(ROUNDS):
        send_rows = send_elem[step_round].reshape(N_DOM, FACES) + home[:, None] * E_LOC
        picked = response[:, :, :, send_rows]
        select = face_select(trace_mats, send_face[step_round].reshape(N_DOM, FACES))
        traced = jnp.einsum('psgb,cjbps->cjgps', select, picked, precision=lax.Precision.HIGHEST)
        partner = jnp.bitwise_xor(home, round_masks[step_round]).astype(jnp.int32)
        received = traced[:, :, :, partner, :]
        lifted = jnp.einsum('bg,cjgps->cjbps', lift_mat, received, precision=lax.Precision.HIGHEST)
        recv_rows = recv_elem[step_round].reshape(N_DOM, FACES) + home[:, None] * E_LOC
        image = image.at[:, :, :, recv_rows.reshape(-1)].add(lifted.reshape(2, NH, NODE_VARS, N_DOM * FACES))
    return image
```

```python
import jax
import jax.numpy as jnp
from jax import lax
from jax.experimental import pallas as pl
from jax.experimental.pallas import tpu as pltpu
from jax.sharding import PartitionSpec as P

REACH = 8
ROUNDS = 4
CHUNKS = 4
base_omega = 0.2

F32 = jnp.float32
BF16 = jnp.bfloat16
VMEM = pl.BlockSpec(memory_space=pltpu.VMEM)
SMEM = pl.BlockSpec(memory_space=pltpu.SMEM)


def split(value):
    high = value.astype(BF16)
    low = (value - high.astype(F32)).astype(BF16)
    return high, low


def dot(a, b):
    return lax.dot_general(a, b, (((1,), (0,)), ((), ())), preferred_element_type=F32)


def dot_nt(a, b):
    return lax.dot_general(a, b, (((1,), (1,)), ((), ())), preferred_element_type=F32)


def round_rows(masks):
    first = jnp.int32(0)
    last = jnp.int32(0)
    for r in range(ROUNDS):
        smallest = masks[r] == 1
        largest = masks[r] == 31
        first = jnp.where(smallest, r, first)
        last = jnp.where(largest, r, last)
    mid_a = jnp.int32(0)
    mid_b = jnp.int32(0)
    for r in range(ROUNDS):
        middle = jnp.logical_and(first != r, last != r)
        mid_b = jnp.where(middle, r, mid_b)
        back = ROUNDS - 1 - r
        middle = jnp.logical_and(first != back, last != back)
        mid_a = jnp.where(middle, back, mid_a)
    return first, last, mid_a, mid_b


def slot_row(ref, rows):
    return jnp.concatenate([ref[pl.ds(r, 1), :] for r in rows], axis=1)


def trace_kernel(masks, response, trace_mats, send_elem, send_face, small, large, middle, lane_masks):
    rows = round_rows(masks)
    elems = slot_row(send_elem, rows)
    faces = slot_row(send_face, rows)
    harm_count, unknowns, elements = response.shape[1:]
    slots = elems.shape[1]
    half = slots // 4
    pick = (lax.broadcasted_iota(jnp.int32, (elements, slots), 0) == elems).astype(F32).astype(BF16)
    mats = trace_mats[...].reshape(-1, unknowns)
    m_high, m_low = split(mats)
    stack = jnp.concatenate([m_high, m_low, m_high], axis=1)
    face_vars = mats.shape[0] // 4
    left = lax.broadcasted_iota(jnp.int32, (face_vars, 2 * half), 1) < half

    def traced(c, j):
        high, low = split(response[c, j])
        p_high = dot(high, pick).astype(BF16)
        p_low = dot(low, pick).astype(BF16)
        out = dot(stack, jnp.concatenate([p_high, p_high, p_low], axis=0))
        total = jnp.zeros((face_vars, slots), F32)
        for face_id in range(4):
            total = total + jnp.where(
                faces == face_id, out[face_id * face_vars:(face_id + 1) * face_vars], 0.0
            )
        return total

    for j in range(harm_count):
        real = traced(0, j)
        imag = traced(1, j)
        ends_r, ends_i = real[:, :2 * half], imag[:, :2 * half]
        small[j] = jnp.where(left, ends_r, pltpu.roll(ends_i, half, 1))
        large[j] = jnp.where(left, pltpu.roll(ends_r, half, 1), ends_i)
        middle[0, j] = real[:, 2 * half:]
        middle[1, j] = imag[:, 2 * half:]
    lane = lax.broadcasted_iota(jnp.int32, lane_masks.shape, 1)
    lane_masks[...] = jnp.where(lane < half, masks[rows[2]], masks[rows[3]])


def tiles(unknowns, elements, body):
    cols = elements // 128
    def step(t, carry):
        r = pl.ds(pl.multiple_of((t // cols) * 8, 8), 8)
        e = pl.ds(pl.multiple_of((t % cols) * 128, 128), 128)
        body(r, e)
        return carry
    lax.fori_loop(0, (unknowns // 8) * cols, step, 0)


def conv_pairs(get_in, coeff, r, e, pairs, acc_r, acc_i):
    for i, m in pairs:
        c_r = coeff[0, m, r, e]
        c_i = coeff[1, m, r, e]
        x_r, x_i = get_in(i)
        acc_r = acc_r + c_r * x_r - c_i * x_i
        acc_i = acc_i + c_r * x_i + c_i * x_r
    return acc_r, acc_i


def high_pairs(j, count):
    return [(i, j - i) for i in range(j + 1)]


def low_pairs(j, count):
    return [(i, 2 * REACH + j - i) for i in range(j, count)]


def own_pairs(j, count):
    return [(i, REACH + j - i) for i in range(count)]


def conv_kernel(response, coeff, *refs):
    chunks, acc = refs[:-1], refs[-1]
    harm_count, unknowns, elements = response.shape[1:]
    odd = lax.axis_index("harm") % 2
    width = chunks[0].shape[1]

    def run(side_pairs):
        def body(r, e):
            own = [(response[0, i, r, e], response[1, i, r, e]) for i in range(harm_count)]
            side = [
                (chunks[i // width][0, i % width, r, e], chunks[i // width][1, i % width, r, e])
                for i in range(harm_count)
            ]
            for j in range(harm_count):
                a = jnp.zeros((8, 128), F32)
                a_r, a_i = conv_pairs(lambda i: own[i], coeff, r, e, own_pairs(j, harm_count), a, a)
                a_r, a_i = conv_pairs(lambda i: side[i], coeff, r, e, side_pairs(j, harm_count), a_r, a_i)
                acc[0, j, r, e] = a_r
                acc[1, j, r, e] = a_i
        tiles(unknowns, elements, body)

    @pl.when(odd == 0)
    def _():
        run(high_pairs)

    @pl.when(odd == 1)
    def _():
        run(low_pairs)


def final_kernel(
    masks, response, coeff, acc, volume_mat, lift_mat, recv_elem, small, large, middle, *refs
):
    chunks, out, conv = refs[:-2], refs[-2], refs[-1]
    harm_count, unknowns, elements = response.shape[1:]
    harm = lax.axis_index("harm")
    odd = harm % 2
    width = chunks[0].shape[1]

    def run(side_pairs):
        def body(r, e):
            side = [
                (chunks[i // width][0, i % width, r, e], chunks[i // width][1, i % width, r, e])
                for i in range(harm_count)
            ]
            for j in range(harm_count):
                a_r, a_i = conv_pairs(
                    lambda i: side[i], coeff, r, e, side_pairs(j, harm_count),
                    acc[0, j, r, e], acc[1, j, r, e],
                )
                conv[0, j, r, e] = a_r
                conv[1, j, r, e] = a_i
        tiles(unknowns, elements, body)

    @pl.when(odd == 0)
    def _():
        run(low_pairs)

    @pl.when(odd == 1)
    def _():
        run(high_pairs)

    rows = round_rows(masks)
    elems = slot_row(recv_elem, rows)
    slots = elems.shape[1]
    half = slots // 4
    place = (lax.broadcasted_iota(jnp.int32, (elements, slots), 0) == elems).astype(F32).astype(BF16)
    v_high, v_low = split(volume_mat[...])
    l_high, l_low = split(lift_mat[...])
    stack = jnp.concatenate([v_high, v_low, v_high, l_high, l_low, l_high], axis=1)
    face_vars = lift_mat.shape[1]
    left = lax.broadcasted_iota(jnp.int32, (face_vars, 2 * half), 1) < half
    period = lax.axis_size("harm") * harm_count
    for j in range(harm_count):
        got_s, got_l = small[j], large[j]
        ends_r = jnp.where(left, got_s, pltpu.roll(got_l, half, 1))
        ends_i = jnp.where(left, pltpu.roll(got_s, half, 1), got_l)
        slot = harm * harm_count + j
        wave = jnp.where(slot < period // 2, slot, slot - period).astype(F32)
        frequency = base_omega * wave
        for c, ends in ((0, ends_r), (1, ends_i)):
            got = jnp.concatenate([ends, middle[c, j]], axis=1)
            g_high, g_low = split(got)
            q = dot_nt(g_high, place) + dot_nt(g_low, place)
            q_high, q_low = split(q)
            x_high, x_low = split(conv[c, j])
            image = dot(stack, jnp.concatenate([x_high, x_high, x_low, q_high, q_high, q_low], axis=0))
            if c == 0:
                out[0, j] = image - frequency * response[1, j]
            else:
                out[1, j] = image + frequency * response[0, j]


def from_partner(value, axis, mask):
    return lax.ppermute(value, axis, [(i, i ^ mask) for i in range(lax.axis_size(axis))])


def local(
    response,
    base_coeff,
    volume_mat,
    trace_mats,
    lift_mat,
    round_masks,
    send_elem,
    send_face,
    recv_elem,
):
    harm_count, unknowns, elements = response.shape[1:]
    groups = lax.axis_size("harm")
    parts = lax.axis_size("dom")
    width = harm_count // CHUNKS
    near, far = [], []
    skip = [(i, (i + 2) % groups if i % 2 == 0 else (i - 2) % groups) for i in range(groups)]
    for k in range(CHUNKS):
        piece = response[:, k * width:(k + 1) * width]
        near.append(from_partner(piece, "harm", 1))
    for k in range(CHUNKS):
        far.append(lax.ppermute(near[k], "harm", skip))

    face_vars = trace_mats.shape[1]
    slots = send_elem.shape[1]
    ends_shape = jax.ShapeDtypeStruct((harm_count, face_vars, 2 * slots), F32)
    small, large, middle, lane_masks = pl.pallas_call(
        trace_kernel,
        name="traces",
        in_specs=[SMEM] + [VMEM] * 4,
        out_specs=[VMEM] * 4,
        out_shape=[
            ends_shape,
            ends_shape,
            jax.ShapeDtypeStruct((2, harm_count, face_vars, 2 * slots), F32),
            jax.ShapeDtypeStruct((1, 2 * slots), jnp.int32),
        ],
    )(round_masks, response, trace_mats, send_elem, send_face)
    small = from_partner(small, "dom", 1)
    large = from_partner(large, "dom", parts - 1)
    for bit in (0, 4, 1, 2, 3):
        swapped = from_partner(middle, "dom", 1 << bit)
        chosen = jnp.bitwise_and(jnp.right_shift(lane_masks, bit), 1) == 1
        middle = jnp.where(chosen[:, None, None], swapped, middle)

    acc = pl.pallas_call(
        conv_kernel,
        name="conv_near",
        in_specs=[VMEM] * (2 + CHUNKS),
        out_specs=VMEM,
        out_shape=jax.ShapeDtypeStruct(response.shape, F32),
    )(response, base_coeff, *near)
    return pl.pallas_call(
        final_kernel,
        name="finish",
        in_specs=[SMEM] + [VMEM] * (9 + CHUNKS),
        out_specs=VMEM,
        out_shape=jax.ShapeDtypeStruct(response.shape, F32),
        scratch_shapes=[pltpu.VMEM(response.shape, F32)],
    )(
        round_masks, response, base_coeff, acc, volume_mat, lift_mat, recv_elem,
        small, large, middle, *far,
    )


def solution(mesh):
    in_specs = (
        P(None, "harm", None, "dom"),
        P(None, None, None, "dom"),
        P(),
        P(),
        P(),
        P(),
        P(None, "dom"),
        P(None, "dom"),
        P(None, "dom"),
    )
    out_specs = P(None, "harm", None, "dom")
    return jax.shard_map(local, mesh=mesh, in_specs=in_specs, out_specs=out_specs, check_vma=False)
```

```python
import jax
import jax.numpy as jnp
from jax import lax
from jax.experimental import pallas as pl
from jax.experimental.pallas import tpu as pltpu
from jax.sharding import PartitionSpec as P


REACH = 8
ROUNDS = 4
WIDTHS = (2, 2, 2, 1, 1)
EARLY = 2
base_omega = 0.2

F32 = jnp.float32
BF16 = jnp.bfloat16
KERNEL_MEMORY = pltpu.CompilerParams(vmem_limit_bytes=8 * 2**20)
HBM = pl.BlockSpec(memory_space=pl.ANY)
VMEM = pl.BlockSpec(memory_space=pltpu.VMEM)
SMEM = pl.BlockSpec(memory_space=pltpu.SMEM)


def split(value):
    high = value.astype(BF16)
    low = (value - high.astype(F32)).astype(BF16)
    return high, low


def dot(a, b):
    return lax.dot_general(a, b, (((1,), (0,)), ((), ())), preferred_element_type=F32)


def dot_nt(a, b):
    return lax.dot_general(a, b, (((1,), (1,)), ((), ())), preferred_element_type=F32)


def round_rows(masks):
    first = jnp.int32(0)
    last = jnp.int32(0)
    for r in range(ROUNDS):
        smallest = masks[r] == 1
        largest = masks[r] == 31
        first = jnp.where(smallest, r, first)
        last = jnp.where(largest, r, last)
    mid_a = jnp.int32(0)
    mid_b = jnp.int32(0)
    for r in range(ROUNDS):
        middle = jnp.logical_and(first != r, last != r)
        mid_b = jnp.where(middle, r, mid_b)
        back = ROUNDS - 1 - r
        middle = jnp.logical_and(first != back, last != back)
        mid_a = jnp.where(middle, back, mid_a)
    return first, last, mid_a, mid_b


def slot_row(ref, rows):
    return jnp.concatenate([ref[pl.ds(r, 1), :] for r in rows], axis=1)


def cut_kernel(response, whole, *refs):
    pieces, sems = refs[:-1], refs[-1]
    odd = lax.axis_index("harm") % 2
    count = response.shape[1]
    copies = []
    for k, piece in enumerate(pieces):
        first = jnp.where(
            odd == 1, chunk_harmonics(k, count, False)[0], chunk_harmonics(k, count, True)[0]
        )
        copies.append(
            pltpu.make_async_copy(response.at[:, pl.ds(first, WIDTHS[k])], piece, sems.at[k])
        )
    copies.append(pltpu.make_async_copy(response, whole, sems.at[len(pieces)]))
    for copy in copies:
        copy.start()
    for copy in copies:
        copy.wait()


def trace_kernel(masks, response, trace_mats, send_elem, send_face, staged, stay_put, large, lane_bits, p_high, p_low):
    rows = round_rows(masks)
    elems = slot_row(send_elem, rows)
    faces = slot_row(send_face, rows)
    harm_count, unknowns, elements = response.shape[1:]
    slots = elems.shape[1]
    half = slots // 4
    pick = (lax.broadcasted_iota(jnp.int32, (elements, slots), 0) == elems).astype(F32).astype(BF16)
    high, low = split(response[...].reshape(-1, elements))
    p_high[...] = dot(high, pick).astype(BF16)
    p_low[...] = dot(low, pick).astype(BF16)
    mats = trace_mats[...].reshape(-1, unknowns)
    m_high, m_low = split(mats)
    stack = jnp.concatenate([m_high, m_low, m_high], axis=1)
    face_vars = mats.shape[0] // 4
    left = lax.broadcasted_iota(jnp.int32, (face_vars, 2 * half), 1) < half

    def traced(c, j):
        at = pl.ds((c * harm_count + j) * unknowns, unknowns)
        top = p_high[at, :]
        out = dot(stack, jnp.concatenate([top, top, p_low[at, :]], axis=0))
        total = jnp.zeros((face_vars, slots), F32)
        for face_id in range(4):
            total = total + jnp.where(
                faces == face_id, out[face_id * face_vars:(face_id + 1) * face_vars], 0.0
            )
        return total

    for j in range(harm_count):
        real = traced(0, j)
        imag = traced(1, j)
        ends_r, ends_i = real[:, :2 * half], imag[:, :2 * half]
        staged[2 * harm_count + j] = jnp.where(left, ends_r, pltpu.roll(ends_i, half, 1))
        large[j] = jnp.where(left, pltpu.roll(ends_r, half, 1), ends_i)
        for row, value in ((j, real), (harm_count + j, imag)):
            staged[row] = value[:, 2 * half:]
            stay_put[row] = value[:, 2 * half:]
    lane = lax.broadcasted_iota(jnp.int32, (1, 2 * half), 1)
    mask = jnp.where(lane < half, masks[rows[2]], masks[rows[3]])
    bits = [jnp.bitwise_and(jnp.right_shift(mask, b), 1) for b in range(5)]
    for row, bit in enumerate((bits[0], bits[1], jnp.bitwise_xor(bits[2], bits[3]), bits[3], bits[4])):
        lane_bits[row:row + 1, :] = bit


def tiles(unknowns, elements, body):
    cols = elements // 128

    def step(t, carry):
        r = pl.ds(pl.multiple_of((t // cols) * 8, 8), 8)
        e = pl.ds(pl.multiple_of((t % cols) * 128, 128), 128)
        body(r, e)
        return carry

    lax.fori_loop(0, (unknowns // 8) * cols, step, 0)


def add_pair(coeff, m, r, e, x, total):
    c_r = coeff[0, m, r, e]
    c_i = coeff[1, m, r, e]
    add_r = c_r * x[0] - c_i * x[1]
    add_i = c_r * x[1] + c_i * x[0]
    if total is None:
        return add_r, add_i
    return total[0] + add_r, total[1] + add_i


def above(i, j):
    return j - i if i <= j else None


def below(i, j):
    return 2 * REACH + j - i if i >= j else None


def inside(i, j):
    return REACH + j - i


def chunk_harmonics(k, count, ascending):
    done = sum(WIDTHS[:k])
    first = done if ascending else count - done - WIDTHS[k]
    return [first + q for q in range(WIDTHS[k])]


def gather_sources(chunks, first, count, ascending, index):
    return [
        (chunk, q, i, index)
        for k, chunk in enumerate(chunks)
        for q, i in enumerate(chunk_harmonics(first + k, count, ascending))
    ]


def convolve(coeff, sources, r, e, start, outputs):
    values = {}
    for j in outputs:
        total = start(j)
        for n, (ref, at, i, index) in enumerate(sources):
            m = index(i, j)
            if m is None:
                continue
            if n not in values:
                values[n] = (ref[0, at, r, e], ref[1, at, r, e])
            total = add_pair(coeff, m, r, e, values[n], total)
        yield j, total


def by_parity(run):
    odd = lax.axis_index("harm") % 2

    @pl.when(odd == 0)
    def _():
        run(False, above, below)

    @pl.when(odd == 1)
    def _():
        run(True, below, above)


def own_kernel(response, coeff, acc):
    harm_count, unknowns, elements = response.shape[1:]
    sources = [(response, i, i, inside) for i in range(harm_count)]

    def body(r, e):
        for j, total in convolve(coeff, sources, r, e, lambda j: None, range(harm_count)):
            acc[0, j, r, e], acc[1, j, r, e] = total

    tiles(unknowns, elements, body)


def near_kernel(first, coeff, acc, *refs):
    chunks, out = refs[:-1], refs[-1]
    harm_count, unknowns, elements = acc.shape[1:]

    def run(ascending, near_index, far_index):
        sources = gather_sources(chunks, first, harm_count, ascending, near_index)

        def body(r, e):
            start = lambda j: (acc[0, j, r, e], acc[1, j, r, e])
            for j, total in convolve(coeff, sources, r, e, start, range(harm_count)):
                out[0, j, r, e], out[1, j, r, e] = total

        tiles(unknowns, elements, body)

    by_parity(run)


def stacked(mat):
    high, low = split(mat)
    return jnp.concatenate([high, low, high], axis=1)


def product(stack, value):
    high, low = split(value)
    return dot(stack, jnp.concatenate([high, high, low], axis=0))


def main_kernel(coeff, acc, volume_mat, *refs):
    chunks, out, conv = refs[:-2], refs[-2], refs[-1]
    harm_count, unknowns, elements = acc.shape[1:]

    def run(ascending, near_index, far_index):
        sources = gather_sources(chunks, 0, harm_count, ascending, far_index)

        def body(r, e):
            start = lambda j: (acc[0, j, r, e], acc[1, j, r, e])
            for j, total in convolve(coeff, sources, r, e, start, range(harm_count)):
                conv[0, j, r, e], conv[1, j, r, e] = total

        tiles(unknowns, elements, body)

    by_parity(run)
    stack = stacked(volume_mat[...])
    for j in range(harm_count):
        for c in range(2):
            out[c, j] = product(stack, conv[c, j])


def lift_kernel(masks, response, image, lift_mat, recv_elem, small, large, middle, out, edge, got):
    harm_count, _, elements = response.shape[1:]
    harm = lax.axis_index("harm")
    rows = round_rows(masks)
    elems = slot_row(recv_elem, rows)
    slots = elems.shape[1]
    half = slots // 4
    place = (lax.broadcasted_iota(jnp.int32, (elements, slots), 0) == elems).astype(F32).astype(BF16)
    face_vars = lift_mat.shape[1]
    left = lax.broadcasted_iota(jnp.int32, (face_vars, 2 * half), 1) < half
    for j in range(harm_count):
        got_s, got_l = small[2 * harm_count + j], large[j]
        for c in range(2):
            at = pl.ds((c * harm_count + j) * face_vars, face_vars)
            if c == 0:
                got[at, :2 * half] = jnp.where(left, got_s, pltpu.roll(got_l, half, 1))
            else:
                got[at, :2 * half] = jnp.where(left, pltpu.roll(got_s, half, 1), got_l)
            got[at, 2 * half:] = middle[c * harm_count + j]
    g_high, g_low = split(got[...])
    placed = dot_nt(g_high, place) + dot_nt(g_low, place)
    got[...] = placed
    stack = stacked(lift_mat[...])
    period = lax.axis_size("harm") * harm_count
    for j in range(harm_count):
        slot = harm * harm_count + j
        wave = jnp.where(slot < period // 2, slot, slot - period).astype(F32)
        frequency = base_omega * wave
        for c in range(2):
            at = pl.ds((c * harm_count + j) * face_vars, face_vars)
            value = image[c, j] + product(stack, got[at, :])
            if c == 0:
                out[0, j] = value - frequency * response[1, j]
            else:
                out[1, j] = value + frequency * response[0, j]
    width = WIDTHS[-1]
    odd = harm % 2
    edge[...] = out[:, pl.ds(odd * (harm_count - width), width)]


def tail_kernel(coeff, volume_mat, edge, chunk, image, out, conv, sem):
    del image
    width, unknowns, elements = edge.shape[1:]
    harm_count = out.shape[1]
    last = len(WIDTHS) - 1

    def run(ascending, near_index, far_index):
        sources = gather_sources([chunk], last, harm_count, ascending, far_index)
        first = harm_count - width if ascending else 0
        outputs = range(first, first + width)

        def body(r, e):
            for j, total in convolve(coeff, sources, r, e, lambda j: None, outputs):
                conv[0, j - first, r, e], conv[1, j - first, r, e] = total

        tiles(unknowns, elements, body)

    by_parity(run)
    stack = stacked(volume_mat[...])
    for q in range(width):
        for c in range(2):
            conv[c, q] = edge[c, q] + product(stack, conv[c, q])
    odd = lax.axis_index("harm") % 2
    copy = pltpu.make_async_copy(conv, out.at[:, pl.ds(odd * (harm_count - width), width)], sem)
    copy.start()
    copy.wait()


def resident(*values):
    return [pltpu.with_memory_space_constraint(value, pltpu.VMEM) for value in values]


def stay(*values):
    return [pltpu.with_memory_space_constraint(value, pltpu.HBM) for value in values]


def resident_shape(shape, dtype=F32):
    return pltpu.VMEM(shape, dtype)


def from_partner(value, axis, mask):
    return lax.ppermute(value, axis, [(i, i ^ mask) for i in range(lax.axis_size(axis))])


def shape_like(value):
    return jax.ShapeDtypeStruct(value.shape, value.dtype)


def local(
    response,
    base_coeff,
    volume_mat,
    trace_mats,
    lift_mat,
    round_masks,
    send_elem,
    send_face,
    recv_elem,
):
    harm_count, unknowns, elements = response.shape[1:]
    groups = lax.axis_size("harm")
    parts = lax.axis_size("dom")
    skip = [(i, (i + 2) % groups if i % 2 == 0 else (i - 2) % groups) for i in range(groups)]
    near, far = [], []
    whole = response
    response, *pieces = pl.pallas_call(
        cut_kernel,
        name="cut",
        compiler_params=KERNEL_MEMORY,
        in_specs=[HBM],
        out_specs=[VMEM] * (1 + len(WIDTHS)),
        out_shape=[resident_shape(response.shape)]
        + [resident_shape((2, width, unknowns, elements)) for width in WIDTHS],
        scratch_shapes=[pltpu.SemaphoreType.DMA((1 + len(WIDTHS),))],
    )(*stay(response))
    (response,) = resident(response)
    for piece in pieces:
        near.append(from_partner(piece, "harm", 1))
    for k in range(len(WIDTHS)):
        far.append(lax.ppermute(near[k], "harm", skip))

    face_vars = trace_mats.shape[1]
    slots = send_elem.shape[1]
    staged, own, large, lane_bits = pl.pallas_call(
        trace_kernel,
        name="traces",
        compiler_params=KERNEL_MEMORY,
        in_specs=[SMEM] + [VMEM] * 4,
        out_specs=[VMEM] * 4,
        out_shape=[
            resident_shape((3 * harm_count, face_vars, 2 * slots), F32),
            resident_shape((2 * harm_count, face_vars, 2 * slots), F32),
            resident_shape((harm_count, face_vars, 2 * slots), F32),
            resident_shape((8, 2 * slots), jnp.int32),
        ],
        scratch_shapes=[pltpu.VMEM((2 * harm_count * unknowns, 4 * slots), BF16)] * 2,
    )(*stay(round_masks), response, *stay(trace_mats, send_elem, send_face))
    large = from_partner(large, "dom", parts - 1)
    bit = lambda row: lane_bits[row] == 1
    small = from_partner(staged, "dom", 1)
    by_two = from_partner(own, "dom", 2)
    by_three = from_partner(own, "dom", 3)
    middle = jnp.where(
        bit(0), jnp.where(bit(1), by_three, small[:2 * harm_count]), jnp.where(bit(1), by_two, own)
    )
    for stage, mask in enumerate((4, 12, 16), 1):
        swapped = from_partner(middle, "dom", mask)
        middle = jnp.where(bit(stage + 1), swapped, middle)

    acc = pl.pallas_call(
        own_kernel,
        name="own",
        compiler_params=KERNEL_MEMORY,
        in_specs=[VMEM] * 2,
        out_specs=VMEM,
        out_shape=resident_shape(response.shape),
    )(response, *resident(base_coeff))

    def near_call(acc, first, chunks):
        return pl.pallas_call(
            lambda *refs: near_kernel(first, *refs),
            name="near",
            compiler_params=KERNEL_MEMORY,
            in_specs=[VMEM] * (2 + len(chunks)),
            out_specs=VMEM,
            out_shape=resident_shape(response.shape),
        )(*resident(base_coeff, acc, *chunks))

    acc = near_call(acc, 0, near[:EARLY])
    acc = near_call(acc, EARLY, near[EARLY:])
    image = pl.pallas_call(
        main_kernel,
        name="main",
        compiler_params=KERNEL_MEMORY,
        in_specs=[VMEM] * (2 + len(WIDTHS)),
        out_specs=VMEM,
        out_shape=resident_shape(response.shape),
        scratch_shapes=[pltpu.VMEM(response.shape, F32)],
    )(*resident(base_coeff, acc), volume_mat, *resident(*far[:-1]))
    width = WIDTHS[-1]
    edge_shape = (2, width, unknowns, elements)
    image, edge = pl.pallas_call(
        lift_kernel,
        name="lift",
        compiler_params=KERNEL_MEMORY,
        in_specs=[SMEM] + [VMEM] * 7,
        out_specs=[VMEM] * 2,
        out_shape=[shape_like(whole), resident_shape(edge_shape, F32)],
        scratch_shapes=[pltpu.VMEM((2 * harm_count * face_vars, elements), F32)],
    )(*stay(round_masks), response, *resident(image), *stay(lift_mat, recv_elem), *resident(small, large, middle))
    return pl.pallas_call(
        tail_kernel,
        name="tail",
        compiler_params=KERNEL_MEMORY,
        in_specs=[VMEM] * 4 + [HBM],
        out_specs=HBM,
        out_shape=shape_like(whole),
        input_output_aliases={4: 0},
        scratch_shapes=[pltpu.VMEM(edge_shape, F32), pltpu.SemaphoreType.DMA],
    )(*resident(base_coeff), volume_mat, *resident(edge, far[-1]), image)


def solution(mesh):
    in_specs = (
        P(None, "harm", None, "dom"),
        P(None, None, None, "dom"),
        P(),
        P(),
        P(),
        P(),
        P(None, "dom"),
        P(None, "dom"),
        P(None, "dom"),
    )
    out_specs = P(None, "harm", None, "dom")

    return jax.shard_map(local, mesh=mesh, in_specs=in_specs, out_specs=out_specs, check_vma=False)
```

```python
import functools

import jax
import jax.numpy as jnp
from jax import lax
from jax.experimental import pallas as pl
from jax.experimental.pallas import tpu as pltpu
from jax.sharding import PartitionSpec as P


REACH = 8
ROUNDS = 4
WIDTHS = (2, 2, 2, 2)
EARLY = 2
base_omega = 0.2

F32 = jnp.float32
BF16 = jnp.bfloat16
KERNEL_MEMORY = pltpu.CompilerParams(vmem_limit_bytes=8 * 2**20)
HBM = pl.BlockSpec(memory_space=pl.ANY)
VMEM = pl.BlockSpec(memory_space=pltpu.VMEM)
SMEM = pl.BlockSpec(memory_space=pltpu.SMEM)


def split(value):
    high = value.astype(BF16)
    low = (value - high.astype(F32)).astype(BF16)
    return high, low


def dot(a, b):
    return lax.dot_general(a, b, (((1,), (0,)), ((), ())), preferred_element_type=F32)


def dot_nt(a, b):
    return lax.dot_general(a, b, (((1,), (1,)), ((), ())), preferred_element_type=F32)


def round_rows(masks):
    first = jnp.int32(0)
    last = jnp.int32(0)
    for r in range(ROUNDS):
        smallest = masks[r] == 1
        largest = masks[r] == 31
        first = jnp.where(smallest, r, first)
        last = jnp.where(largest, r, last)
    mid_a = jnp.int32(0)
    mid_b = jnp.int32(0)
    for r in range(ROUNDS):
        middle = jnp.logical_and(first != r, last != r)
        mid_b = jnp.where(middle, r, mid_b)
        back = ROUNDS - 1 - r
        middle = jnp.logical_and(first != back, last != back)
        mid_a = jnp.where(middle, back, mid_a)
    return first, last, mid_a, mid_b


def slot_row(ref, rows):
    return jnp.concatenate([ref[pl.ds(r, 1), :] for r in rows], axis=1)


def piece_copy(response, k, piece, sem):
    count = response.shape[1]
    odd = lax.axis_index("harm") % 2
    upward, downward = (chunk_harmonics(k, count, way)[0] for way in (True, False))
    first = jnp.where(odd == 1, downward, upward)
    return pltpu.make_async_copy(response.at[:, pl.ds(first, WIDTHS[k])], piece, sem)


def cut_kernel(response, piece, sem):
    copy = piece_copy(response, 0, piece, sem)
    copy.start()
    copy.wait()


def trace_kernel(masks_hbm, response_hbm, coeff_hbm, mats_hbm, elem_hbm, face_hbm, recv_hbm, *refs):
    count = len(WIDTHS) - 1
    first, lane_bits, places, response, coeff = refs[:5]
    pieces = refs[5:5 + count]
    p_high, p_low, masks, trace_mats, send_elem, send_face, recv_elem, sems = refs[5 + count:]
    fetched = (
        (response_hbm, response), (masks_hbm, masks), (elem_hbm, send_elem), (face_hbm, send_face),
        (mats_hbm, trace_mats), (recv_hbm, recv_elem),
    )
    fetches = [
        pltpu.make_async_copy(source, target, sems.at[n]) for n, (source, target) in enumerate(fetched)
    ]
    copies = [
        piece_copy(response_hbm, k, piece, sems.at[len(fetched) + k])
        for k, piece in enumerate(pieces, 1)
    ]
    copies.append(pltpu.make_async_copy(coeff_hbm, coeff, sems.at[len(fetched)]))
    for copy in fetches + copies:
        copy.start()
    for copy in fetches[1:]:
        copy.wait()
    rows = round_rows(masks)
    elems = slot_row(send_elem, rows)
    faces = slot_row(send_face, rows)
    places[0:1, :] = slot_row(recv_elem, rows)
    harm_count, unknowns, elements = response.shape[1:]
    slots = elems.shape[1]
    half = slots // 4
    pick = (lax.broadcasted_iota(jnp.int32, (elements, slots), 0) == elems).astype(F32).astype(BF16)
    mats = trace_mats[...].reshape(-1, unknowns)
    m_high, m_low = split(mats)
    stack = jnp.concatenate([m_high, m_low, m_high], axis=1)
    face_vars = mats.shape[0] // 4
    left = lax.broadcasted_iota(jnp.int32, (face_vars, 2 * half), 1) < half
    for n, row in enumerate(rows[2:]):
        mask = jnp.full((1, 2 * half), masks[row], jnp.int32)
        bits = [jnp.bitwise_and(jnp.right_shift(mask, b), 1) for b in range(5)]
        bits[2] = jnp.bitwise_xor(bits[2], bits[3])
        for b, bit in enumerate(bits):
            lane_bits[8 * n + b:8 * n + b + 1, :] = bit
    fetches[0].wait()
    high, low = split(response[...].reshape(-1, elements))
    p_high[...] = dot(high, pick).astype(BF16)
    p_low[...] = dot(low, pick).astype(BF16)

    def traced(c, j):
        at = pl.ds((c * harm_count + j) * unknowns, unknowns)
        top = p_high[at, :]
        out = dot(stack, jnp.concatenate([top, top, p_low[at, :]], axis=0))
        total = jnp.zeros((face_vars, slots), F32)
        for face_id in range(4):
            total = total + jnp.where(
                faces == face_id, out[face_id * face_vars:(face_id + 1) * face_vars], 0.0
            )
        return total

    for j in range(harm_count):
        real = traced(0, j)
        imag = traced(1, j)
        ends_r, ends_i = real[:, :2 * half], imag[:, :2 * half]
        mid_r, mid_i = real[:, 2 * half:], imag[:, 2 * half:]
        first[j] = jnp.where(left, mid_r, pltpu.roll(mid_i, half, 1))
        first[harm_count + j] = jnp.where(left, pltpu.roll(mid_r, half, 1), mid_i)
        first[2 * harm_count + j] = jnp.where(left, ends_r, pltpu.roll(ends_i, half, 1))
        first[3 * harm_count + j] = jnp.where(left, pltpu.roll(ends_r, half, 1), ends_i)
    for copy in copies:
        copy.wait()


def choose(lane_bits, chain, row, swapped, kept):
    bit = lane_bits[8 * chain + row:8 * chain + row + 1, :] == 1
    return jnp.where(bit, swapped, kept)


def split_kernel(lane_bits, swapped, kept, out_x, out_y):
    count = out_y.shape[0]
    for n in range(count):
        out_x[n] = choose(lane_bits, 0, 0, swapped[n], kept[n])
        out_y[n] = choose(lane_bits, 1, 0, swapped[count + n], kept[count + n])
    out_x[count:] = swapped[3 * count:]


def first_x_kernel(row, lane_bits, swapped, kept, out, rider):
    count = out.shape[0]
    for n in range(count):
        out[n] = choose(lane_bits, 0, row, swapped[n], kept[n])
    rider[...] = swapped[count:]


def second_x_kernel(row, lane_bits, swapped, kept, rider, out):
    count = kept.shape[0]
    for n in range(count):
        out[n] = choose(lane_bits, 0, row, swapped[n], kept[n])
    out[count:] = rider[...]


def y_kernel(row, lane_bits, swapped, kept, out):
    for n in range(kept.shape[0]):
        out[n] = choose(lane_bits, 1, row, swapped[n], kept[n])


def join_kernel(rows, lane_bits, swapped_x, kept_x, swapped_y, kept_y, out):
    count = kept_y.shape[0]
    for n in range(count):
        out[n] = choose(lane_bits, 0, rows[0], swapped_x[n], kept_x[n])
        out[count + n] = choose(lane_bits, 1, rows[1], swapped_y[n], kept_y[n])
    out[2 * count:] = swapped_x[count:]


def tiles(unknowns, elements, body):
    cols = elements // 128

    def step(t, carry):
        r = pl.ds(pl.multiple_of((t // cols) * 8, 8), 8)
        e = pl.ds(pl.multiple_of((t % cols) * 128, 128), 128)
        body(r, e)
        return carry

    lax.fori_loop(0, (unknowns // 8) * cols, step, 0)


def add_pair(coeff, m, r, e, x, total):
    c_r = coeff[0, m, r, e]
    c_i = coeff[1, m, r, e]
    add_r = c_r * x[0] - c_i * x[1]
    add_i = c_r * x[1] + c_i * x[0]
    if total is None:
        return add_r, add_i
    return total[0] + add_r, total[1] + add_i


def above(i, j):
    return j - i if i <= j else None


def below(i, j):
    return 2 * REACH + j - i if i >= j else None


def inside(i, j):
    return REACH + j - i


def chunk_harmonics(k, count, ascending):
    done = sum(WIDTHS[:k])
    first = done if ascending else count - done - WIDTHS[k]
    return [first + q for q in range(WIDTHS[k])]


def gather_sources(chunks, first, count, ascending, index):
    return [
        (chunk, q, i, index)
        for k, chunk in enumerate(chunks)
        for q, i in enumerate(chunk_harmonics(first + k, count, ascending))
    ]


def convolve(coeff, sources, r, e, start, outputs):
    values = {}
    for j in outputs:
        total = start(j)
        for n, (ref, at, i, index) in enumerate(sources):
            m = index(i, j)
            if m is None:
                continue
            if n not in values:
                values[n] = (ref[0, at, r, e], ref[1, at, r, e])
            total = add_pair(coeff, m, r, e, values[n], total)
        yield j, total


def by_parity(run):
    odd = lax.axis_index("harm") % 2

    @pl.when(odd == 0)
    def _():
        run(False, above, below)

    @pl.when(odd == 1)
    def _():
        run(True, below, above)


def own_kernel(response, coeff, acc):
    harm_count, unknowns, elements = response.shape[1:]
    sources = [(response, i, i, inside) for i in range(harm_count)]

    def body(r, e):
        for j, total in convolve(coeff, sources, r, e, lambda j: None, range(harm_count)):
            acc[0, j, r, e], acc[1, j, r, e] = total

    tiles(unknowns, elements, body)


def near_kernel(first, coeff, acc, *refs):
    chunks, out = refs[:-1], refs[-1]
    harm_count, unknowns, elements = acc.shape[1:]

    def run(ascending, near_index, far_index):
        sources = gather_sources(chunks, first, harm_count, ascending, near_index)

        def body(r, e):
            start = lambda j: (acc[0, j, r, e], acc[1, j, r, e])
            for j, total in convolve(coeff, sources, r, e, start, range(harm_count)):
                out[0, j, r, e], out[1, j, r, e] = total

        tiles(unknowns, elements, body)

    by_parity(run)


def stacked(mat):
    high, low = split(mat)
    return jnp.concatenate([high, low, high], axis=1)


def product(stack, value):
    high, low = split(value)
    return dot(stack, jnp.concatenate([high, high, low], axis=0))


def main_kernel(coeff, response, acc, volume_mat, *refs):
    chunks, out, conv = refs[:-2], refs[-2], refs[-1]
    harm_count, unknowns, elements = acc.shape[1:]

    def run(ascending, near_index, far_index):
        sources = gather_sources(chunks, 0, harm_count, ascending, far_index)

        def body(r, e):
            start = lambda j: (acc[0, j, r, e], acc[1, j, r, e])
            for j, total in convolve(coeff, sources, r, e, start, range(harm_count)):
                conv[0, j, r, e], conv[1, j, r, e] = total

        tiles(unknowns, elements, body)

    by_parity(run)
    stack = stacked(volume_mat[...])
    harm = lax.axis_index("harm")
    period = lax.axis_size("harm") * harm_count
    for j in range(harm_count):
        slot = harm * harm_count + j
        wave = jnp.where(slot < period // 2, slot, slot - period).astype(F32)
        frequency = base_omega * wave
        out[0, j] = product(stack, conv[0, j]) - frequency * response[1, j]
        out[1, j] = product(stack, conv[1, j]) + frequency * response[0, j]


def lift_kernel(
    image, lift_rows, places, lane_bits, small, swapped, kept,
    out, got, done, sems,
):
    harm_count, _, elements = image.shape[1:]
    elems = places[0:1, :]
    slots = elems.shape[1]
    half = slots // 4
    place = (lax.broadcasted_iota(jnp.int32, (elements, slots), 0) == elems).astype(F32).astype(BF16)
    face_vars = lift_rows.shape[0]
    left = lax.broadcasted_iota(jnp.int32, (face_vars, 2 * half), 1) < half
    for j in range(harm_count):
        a = choose(lane_bits, 0, 4, swapped[j], kept[j])
        b = choose(lane_bits, 1, 4, swapped[harm_count + j], kept[harm_count + j])
        for first, second, lanes in (
            (small[2 * harm_count + j], swapped[2 * harm_count + j], slice(0, 2 * half)), (a, b, slice(2 * half, slots))
        ):
            got[pl.ds(j * face_vars, face_vars), lanes] = jnp.where(
                left, first, pltpu.roll(second, half, 1)
            )
            got[pl.ds((harm_count + j) * face_vars, face_vars), lanes] = jnp.where(
                left, pltpu.roll(first, half, 1), second
            )
    g_high, g_low = split(got[...])
    got[...] = dot_nt(g_high, place) + dot_nt(g_low, place)
    l_high, l_low = split(lift_rows[...])
    stack = jnp.concatenate([l_high, l_low, l_high], axis=0)
    copies = []
    for j in range(harm_count):
        for c in range(2):
            at = pl.ds((c * harm_count + j) * face_vars, face_vars)
            q_high, q_low = split(got[at, :])
            done[c, j] = image[c, j] + lax.dot_general(
                stack, jnp.concatenate([q_high, q_high, q_low], axis=0),
                (((0,), (0,)), ((), ())), preferred_element_type=F32,
            )
        copies.append(pltpu.make_async_copy(done.at[:, pl.ds(j, 1)], out.at[:, pl.ds(j, 1)], sems.at[j]))
        copies[-1].start()
    for copy in copies:
        copy.wait()


def edge_kernel(coeff, volume_mat, chunk, image, out, conv):
    width, unknowns, elements = chunk.shape[1:]
    harm_count = out.shape[1]
    last = len(WIDTHS) - 1
    stack = stacked(volume_mat[...])

    def run(ascending, near_index, far_index):
        sources = gather_sources([chunk], last, harm_count, ascending, far_index)
        first = harm_count - width if ascending else 0
        outputs = range(first, first + width)

        def body(r, e):
            for j, total in convolve(coeff, sources, r, e, lambda j: None, outputs):
                conv[0, j - first, r, e], conv[1, j - first, r, e] = total

        tiles(unknowns, elements, body)
        for q in range(width):
            for c in range(2):
                out[c, first + q] = image[c, first + q] + product(stack, conv[c, q])

    by_parity(run)


def resident(*values):
    return [pltpu.with_memory_space_constraint(value, pltpu.VMEM) for value in values]


def stay(*values):
    return [pltpu.with_memory_space_constraint(value, pltpu.HBM) for value in values]


def resident_shape(shape, dtype=F32):
    return pltpu.VMEM(shape, dtype)


def from_partner(value, axis, mask):
    return lax.ppermute(value, axis, [(i, i ^ mask) for i in range(lax.axis_size(axis))])


def shape_like(value):
    return jax.ShapeDtypeStruct(value.shape, value.dtype)


def local(
    response,
    base_coeff,
    volume_mat,
    trace_mats,
    lift_mat,
    round_masks,
    send_elem,
    send_face,
    recv_elem,
):
    harm_count, unknowns, elements = response.shape[1:]
    groups = lax.axis_size("harm")
    skip = [(i, (i + 2) % groups if i % 2 == 0 else (i - 2) % groups) for i in range(groups)]
    near, far = [], []
    whole = response
    face_vars = trace_mats.shape[1]
    slots = send_elem.shape[1]
    piece = pl.pallas_call(
        cut_kernel,
        name="cut",
        compiler_params=KERNEL_MEMORY,
        in_specs=[HBM],
        out_specs=VMEM,
        out_shape=resident_shape((2, WIDTHS[0], unknowns, elements)),
        scratch_shapes=[pltpu.SemaphoreType.DMA],
    )(*stay(response))
    later = len(WIDTHS) - 1
    first, lane_bits, places, response, base_coeff, *pieces = pl.pallas_call(
        trace_kernel,
        name="traces",
        compiler_params=KERNEL_MEMORY,
        in_specs=[HBM] * 7,
        out_specs=[VMEM] * (5 + later),
        out_shape=[
            resident_shape((4 * harm_count, face_vars, 2 * slots)),
            resident_shape((16, 2 * slots), jnp.int32),
            resident_shape((8, 4 * slots), jnp.int32),
            resident_shape(response.shape),
            resident_shape(base_coeff.shape),
        ]
        + [resident_shape((2, width, unknowns, elements)) for width in WIDTHS[1:]],
        scratch_shapes=[pltpu.VMEM((2 * harm_count * unknowns, 4 * slots), BF16)] * 2
        + [pltpu.SMEM(round_masks.shape, jnp.int32), pltpu.VMEM(trace_mats.shape, F32)]
        + [pltpu.VMEM(send_elem.shape, jnp.int32)] * 3
        + [pltpu.SemaphoreType.DMA((7 + later,))],
    )(*stay(round_masks, response, base_coeff, trace_mats, send_elem, send_face, recv_elem))
    for value in [piece, *pieces]:
        near.append(from_partner(value, "harm", 1))
    for k in range(len(WIDTHS)):
        far.append(lax.ppermute(near[k], "harm", skip))

    small = from_partner(first, "dom", 1)

    def choice(kernel, rows, *values):
        shapes = [resident_shape((n * harm_count, face_vars, 2 * slots)) for n in rows]
        return pl.pallas_call(
            kernel,
            name="choice",
            compiler_params=KERNEL_MEMORY,
            in_specs=[VMEM] * (1 + len(values)),
            out_specs=[VMEM] * len(rows),
            out_shape=shapes,
        )(*resident(lane_bits, *values))

    def stage(value, mask):
        return from_partner(value, "dom", mask)

    part = functools.partial
    kept_x, kept_y = choice(split_kernel, (2, 1), small, first)
    moved_x = stage(kept_x, 2)
    moved_y = stage(kept_y, 12)
    kept_x, rider = choice(part(first_x_kernel, 1), (1, 1), moved_x, kept_x)
    moved_x = stage(kept_x, 4)
    (kept_y,) = choice(part(y_kernel, 3), (1,), moved_y, kept_y)
    moved_y = stage(kept_y, 2)
    (kept_x,) = choice(part(second_x_kernel, 2), (2,), moved_x, kept_x, rider)
    moved_x = stage(kept_x, 12)
    (kept_y,) = choice(part(y_kernel, 1), (1,), moved_y, kept_y)
    moved_y = stage(kept_y, 4)
    (kept,) = choice(part(join_kernel, (3, 2)), (3,), moved_x, kept_x, moved_y, kept_y)
    swapped = stage(kept, 16)

    acc = pl.pallas_call(
        own_kernel,
        name="own",
        compiler_params=KERNEL_MEMORY,
        in_specs=[VMEM] * 2,
        out_specs=VMEM,
        out_shape=resident_shape(response.shape),
    )(*resident(response, base_coeff))

    def near_call(acc, first, chunks):
        return pl.pallas_call(
            lambda *refs: near_kernel(first, *refs),
            name="near",
            compiler_params=KERNEL_MEMORY,
            in_specs=[VMEM] * (2 + len(chunks)),
            out_specs=VMEM,
            out_shape=resident_shape(response.shape),
        )(*resident(base_coeff, acc, *chunks))

    acc = near_call(acc, 0, near[:EARLY])
    acc = near_call(acc, EARLY, near[EARLY:])
    image = pl.pallas_call(
        main_kernel,
        name="main",
        compiler_params=KERNEL_MEMORY,
        in_specs=[VMEM] * (3 + len(WIDTHS)),
        out_specs=VMEM,
        out_shape=resident_shape(response.shape),
        scratch_shapes=[pltpu.VMEM(response.shape, F32)],
    )(*resident(base_coeff, response, acc), volume_mat, *resident(*far[:-1]))
    edge_shape = (2, WIDTHS[-1], unknowns, elements)
    image = pl.pallas_call(
        edge_kernel,
        name="edge",
        compiler_params=KERNEL_MEMORY,
        in_specs=[VMEM] * 4,
        out_specs=VMEM,
        out_shape=resident_shape(response.shape),
        input_output_aliases={3: 0},
        scratch_shapes=[pltpu.VMEM(edge_shape, F32)],
    )(*resident(base_coeff), volume_mat, *resident(far[-1], image))
    return pl.pallas_call(
        lift_kernel,
        name="lift",
        compiler_params=KERNEL_MEMORY,
        in_specs=[VMEM] * 7,
        out_specs=HBM,
        out_shape=shape_like(whole),
        scratch_shapes=[
            pltpu.VMEM((2 * harm_count * face_vars, elements), F32),
            pltpu.VMEM(response.shape, F32),
            pltpu.SemaphoreType.DMA((harm_count,)),
        ],
    )(
        *resident(image), lift_mat.T, *resident(places, lane_bits, small, swapped, kept),
    )


def solution(mesh):
    in_specs = (
        P(None, "harm", None, "dom"),
        P(None, None, None, "dom"),
        P(),
        P(),
        P(),
        P(),
        P(None, "dom"),
        P(None, "dom"),
        P(None, "dom"),
    )
    out_specs = P(None, "harm", None, "dom")

    return jax.shard_map(local, mesh=mesh, in_specs=in_specs, out_specs=out_specs, check_vma=False)
```

```python
import functools

import jax
import jax.numpy as jnp
from jax import lax
from jax.experimental import pallas as pl
from jax.experimental.pallas import tpu as pltpu
from jax.sharding import PartitionSpec as P


REACH = 8
ROUNDS = 4
WIDTHS = (2, 2, 2, 2)
FAR_WIDTHS = (2, 2, 2, 1, 1)
FAR_EARLY = 3
EARLY = 2
base_omega = 0.2

F32 = jnp.float32
BF16 = jnp.bfloat16
KERNEL_MEMORY = pltpu.CompilerParams(vmem_limit_bytes=8 * 2**20)
HBM = pl.BlockSpec(memory_space=pl.ANY)
VMEM = pl.BlockSpec(memory_space=pltpu.VMEM)
SMEM = pl.BlockSpec(memory_space=pltpu.SMEM)


def split(value):
    high = value.astype(BF16)
    low = (value - high.astype(F32)).astype(BF16)
    return high, low


def dot(a, b):
    return lax.dot_general(a, b, (((1,), (0,)), ((), ())), preferred_element_type=F32)


def dot_nt(a, b):
    return lax.dot_general(a, b, (((1,), (1,)), ((), ())), preferred_element_type=F32)


def round_rows(masks):
    first = jnp.int32(0)
    last = jnp.int32(0)
    for r in range(ROUNDS):
        smallest = masks[r] == 1
        largest = masks[r] == 31
        first = jnp.where(smallest, r, first)
        last = jnp.where(largest, r, last)
    mid_a = jnp.int32(0)
    mid_b = jnp.int32(0)
    for r in range(ROUNDS):
        middle = jnp.logical_and(first != r, last != r)
        mid_b = jnp.where(middle, r, mid_b)
        back = ROUNDS - 1 - r
        middle = jnp.logical_and(first != back, last != back)
        mid_a = jnp.where(middle, back, mid_a)
    return first, last, mid_a, mid_b


def slot_row(ref, rows):
    return jnp.concatenate([ref[pl.ds(r, 1), :] for r in rows], axis=1)


def piece_copy(response, k, piece, sem, widths=WIDTHS):
    count = response.shape[1]
    odd = lax.axis_index("harm") % 2
    upward, downward = (chunk_harmonics(k, count, way, widths)[0] for way in (True, False))
    first = jnp.where(odd == 1, downward, upward)
    return pltpu.make_async_copy(response.at[:, pl.ds(first, widths[k])], piece, sem)


def cut_kernel(response, piece, sem):
    copy = piece_copy(response, 0, piece, sem)
    copy.start()
    copy.wait()


def relay_kernel(chunk, out):
    odd = lax.axis_index("harm") % 2
    out[...] = chunk[:, pl.ds(1 - odd, 1)]


def trace_kernel(masks_hbm, response_hbm, coeff_hbm, mats_hbm, elem_hbm, face_hbm, recv_hbm, *refs):
    count = len(WIDTHS) - 1
    first, lane_bits, places, response, coeff, direct = refs[:6]
    pieces = refs[6:6 + count]
    p_high, p_low, masks, trace_mats, send_elem, send_face, recv_elem, sems = refs[6 + count:]
    fetched = (
        (response_hbm, response), (masks_hbm, masks), (elem_hbm, send_elem), (face_hbm, send_face),
        (mats_hbm, trace_mats), (recv_hbm, recv_elem),
    )
    fetches = [
        pltpu.make_async_copy(source, target, sems.at[n]) for n, (source, target) in enumerate(fetched)
    ]
    copies = [
        piece_copy(response_hbm, k, piece, sems.at[len(fetched) + k])
        for k, piece in enumerate(pieces, 1)
    ]
    copies.append(pltpu.make_async_copy(coeff_hbm, coeff, sems.at[len(fetched)]))
    copies.append(
        piece_copy(
            response_hbm, len(FAR_WIDTHS) - 1, direct, sems.at[len(fetched) + count + 1], FAR_WIDTHS
        )
    )
    for copy in fetches + copies:
        copy.start()
    for copy in fetches[1:]:
        copy.wait()
    rows = round_rows(masks)
    elems = slot_row(send_elem, rows)
    faces = slot_row(send_face, rows)
    places[0:1, :] = slot_row(recv_elem, rows)
    harm_count, unknowns, elements = response.shape[1:]
    slots = elems.shape[1]
    half = slots // 4
    pick = (lax.broadcasted_iota(jnp.int32, (elements, slots), 0) == elems).astype(F32).astype(BF16)
    mats = trace_mats[...].reshape(-1, unknowns)
    m_high, m_low = split(mats)
    stack = jnp.concatenate([m_high, m_low, m_high], axis=1)
    face_vars = mats.shape[0] // 4
    left = lax.broadcasted_iota(jnp.int32, (face_vars, 2 * half), 1) < half
    for n, row in enumerate(rows[2:]):
        mask = jnp.full((1, 2 * half), masks[row], jnp.int32)
        bits = [jnp.bitwise_and(jnp.right_shift(mask, b), 1) for b in range(5)]
        bits[2] = jnp.bitwise_xor(bits[2], bits[3])
        for b, bit in enumerate(bits):
            lane_bits[8 * n + b:8 * n + b + 1, :] = bit
    fetches[0].wait()
    high, low = split(response[...].reshape(-1, elements))
    p_high[...] = dot(high, pick).astype(BF16)
    p_low[...] = dot(low, pick).astype(BF16)

    def traced(c, j):
        at = pl.ds((c * harm_count + j) * unknowns, unknowns)
        top = p_high[at, :]
        out = dot(stack, jnp.concatenate([top, top, p_low[at, :]], axis=0))
        total = jnp.zeros((face_vars, slots), F32)
        for face_id in range(4):
            total = total + jnp.where(
                faces == face_id, out[face_id * face_vars:(face_id + 1) * face_vars], 0.0
            )
        return total

    for j in range(harm_count):
        real = traced(0, j)
        imag = traced(1, j)
        ends_r, ends_i = real[:, :2 * half], imag[:, :2 * half]
        mid_r, mid_i = real[:, 2 * half:], imag[:, 2 * half:]
        first[j] = jnp.where(left, mid_r, pltpu.roll(mid_i, half, 1))
        first[harm_count + j] = jnp.where(left, pltpu.roll(mid_r, half, 1), mid_i)
        first[2 * harm_count + j] = jnp.where(left, ends_r, pltpu.roll(ends_i, half, 1))
        first[3 * harm_count + j] = jnp.where(left, pltpu.roll(ends_r, half, 1), ends_i)
    for copy in copies:
        copy.wait()


def choose(lane_bits, chain, row, swapped, kept):
    bit = lane_bits[8 * chain + row:8 * chain + row + 1, :] == 1
    return jnp.where(bit, swapped, kept)


def split_kernel(lane_bits, swapped, kept, out_x, out_y):
    count = out_y.shape[0]
    for n in range(count):
        out_x[n] = choose(lane_bits, 0, 0, swapped[n], kept[n])
        out_y[n] = choose(lane_bits, 1, 0, swapped[count + n], kept[count + n])
    out_x[count:] = swapped[3 * count:]


def first_x_kernel(row, lane_bits, swapped, kept, out, rider):
    count = out.shape[0]
    for n in range(count):
        out[n] = choose(lane_bits, 0, row, swapped[n], kept[n])
    rider[...] = swapped[count:]


def second_x_kernel(row, lane_bits, swapped, kept, rider, out):
    count = kept.shape[0]
    for n in range(count):
        out[n] = choose(lane_bits, 0, row, swapped[n], kept[n])
    out[count:] = rider[...]


def y_kernel(row, lane_bits, swapped, kept, out):
    for n in range(kept.shape[0]):
        out[n] = choose(lane_bits, 1, row, swapped[n], kept[n])


def join_kernel(rows, lane_bits, swapped_x, kept_x, swapped_y, kept_y, out):
    count = kept_y.shape[0]
    for n in range(count):
        out[n] = choose(lane_bits, 0, rows[0], swapped_x[n], kept_x[n])
        out[count + n] = choose(lane_bits, 1, rows[1], swapped_y[n], kept_y[n])
    out[2 * count:] = swapped_x[count:]


def tiles(unknowns, elements, body):
    cols = elements // 128

    def step(t, carry):
        r = pl.ds(pl.multiple_of((t // cols) * 8, 8), 8)
        e = pl.ds(pl.multiple_of((t % cols) * 128, 128), 128)
        body(r, e)
        return carry

    lax.fori_loop(0, (unknowns // 8) * cols, step, 0)


def add_pair(coeff, m, r, e, x, total):
    c_r = coeff[0, m, r, e]
    c_i = coeff[1, m, r, e]
    add_r = c_r * x[0] - c_i * x[1]
    add_i = c_r * x[1] + c_i * x[0]
    if total is None:
        return add_r, add_i
    return total[0] + add_r, total[1] + add_i


def above(i, j):
    return j - i if i <= j else None


def below(i, j):
    return 2 * REACH + j - i if i >= j else None


def inside(i, j):
    return REACH + j - i


def chunk_harmonics(k, count, ascending, widths=WIDTHS):
    done = sum(widths[:k])
    first = done if ascending else count - done - widths[k]
    return [first + q for q in range(widths[k])]


def gather_sources(chunks, first, count, ascending, index, widths):
    return [
        (chunk, q, i, index)
        for k, chunk in enumerate(chunks)
        for q, i in enumerate(chunk_harmonics(first + k, count, ascending, widths))
    ]


def convolve(coeff, sources, r, e, start, outputs):
    values = {}
    for j in outputs:
        total = start(j)
        for n, (ref, at, i, index) in enumerate(sources):
            m = index(i, j)
            if m is None:
                continue
            if n not in values:
                values[n] = (ref[0, at, r, e], ref[1, at, r, e])
            total = add_pair(coeff, m, r, e, values[n], total)
        yield j, total


def by_parity(run):
    odd = lax.axis_index("harm") % 2

    @pl.when(odd == 0)
    def _():
        run(False, above, below)

    @pl.when(odd == 1)
    def _():
        run(True, below, above)


def own_kernel(response, coeff, acc):
    harm_count, unknowns, elements = response.shape[1:]
    sources = [(response, i, i, inside) for i in range(harm_count)]

    def body(r, e):
        for j, total in convolve(coeff, sources, r, e, lambda j: None, range(harm_count)):
            acc[0, j, r, e], acc[1, j, r, e] = total

    tiles(unknowns, elements, body)


def near_kernel(first, coeff, acc, *refs):
    chunks, out = refs[:-1], refs[-1]
    harm_count, unknowns, elements = acc.shape[1:]

    def run(ascending, near_index, far_index):
        sources = gather_sources(chunks, first, harm_count, ascending, near_index, WIDTHS)

        def body(r, e):
            start = lambda j: (acc[0, j, r, e], acc[1, j, r, e])
            for j, total in convolve(coeff, sources, r, e, start, range(harm_count)):
                out[0, j, r, e], out[1, j, r, e] = total

        tiles(unknowns, elements, body)

    by_parity(run)


def stacked(mat):
    high, low = split(mat)
    return jnp.concatenate([high, low, high], axis=1)


def product(stack, value):
    high, low = split(value)
    return dot(stack, jnp.concatenate([high, high, low], axis=0))


def main_kernel(coeff, response, acc, volume_mat, *refs):
    chunks, out, conv = refs[:-2], refs[-2], refs[-1]
    harm_count, unknowns, elements = acc.shape[1:]

    def run(ascending, near_index, far_index):
        sources = gather_sources(chunks, 0, harm_count, ascending, far_index, FAR_WIDTHS)

        def body(r, e):
            start = lambda j: (acc[0, j, r, e], acc[1, j, r, e])
            for j, total in convolve(coeff, sources, r, e, start, range(harm_count)):
                conv[0, j, r, e], conv[1, j, r, e] = total

        tiles(unknowns, elements, body)

    by_parity(run)
    stack = stacked(volume_mat[...])
    harm = lax.axis_index("harm")
    period = lax.axis_size("harm") * harm_count
    for j in range(harm_count):
        slot = harm * harm_count + j
        wave = jnp.where(slot < period // 2, slot, slot - period).astype(F32)
        frequency = base_omega * wave
        out[0, j] = product(stack, conv[0, j]) - frequency * response[1, j]
        out[1, j] = product(stack, conv[1, j]) + frequency * response[0, j]


def lift_kernel(
    image, lift_rows, places, lane_bits, small, swapped, kept,
    out, got, done, sems,
):
    harm_count, _, elements = image.shape[1:]
    elems = places[0:1, :]
    slots = elems.shape[1]
    half = slots // 4
    place = (lax.broadcasted_iota(jnp.int32, (elements, slots), 0) == elems).astype(F32).astype(BF16)
    face_vars = lift_rows.shape[0]
    left = lax.broadcasted_iota(jnp.int32, (face_vars, 2 * half), 1) < half
    for j in range(harm_count):
        a = choose(lane_bits, 0, 4, swapped[j], kept[j])
        b = choose(lane_bits, 1, 4, swapped[harm_count + j], kept[harm_count + j])
        for first, second, lanes in (
            (small[2 * harm_count + j], swapped[2 * harm_count + j], slice(0, 2 * half)), (a, b, slice(2 * half, slots))
        ):
            got[pl.ds(j * face_vars, face_vars), lanes] = jnp.where(
                left, first, pltpu.roll(second, half, 1)
            )
            got[pl.ds((harm_count + j) * face_vars, face_vars), lanes] = jnp.where(
                left, pltpu.roll(first, half, 1), second
            )
    g_high, g_low = split(got[...])
    got[...] = dot_nt(g_high, place) + dot_nt(g_low, place)
    l_high, l_low = split(lift_rows[...])
    stack = jnp.concatenate([l_high, l_low, l_high], axis=0)
    copies = []
    for j in range(harm_count):
        for c in range(2):
            at = pl.ds((c * harm_count + j) * face_vars, face_vars)
            q_high, q_low = split(got[at, :])
            done[c, j] = image[c, j] + lax.dot_general(
                stack, jnp.concatenate([q_high, q_high, q_low], axis=0),
                (((0,), (0,)), ((), ())), preferred_element_type=F32,
            )
        copies.append(pltpu.make_async_copy(done.at[:, pl.ds(j, 1)], out.at[:, pl.ds(j, 1)], sems.at[j]))
        copies[-1].start()
    for copy in copies:
        copy.wait()


def edge_kernel(coeff, volume_mat, relayed, direct, image, out, conv):
    width, unknowns, elements = conv.shape[1:]
    harm_count = out.shape[1]
    stack = stacked(volume_mat[...])

    def run(ascending, near_index, far_index):
        sources = gather_sources(
            [relayed, direct], FAR_EARLY, harm_count, ascending, far_index, FAR_WIDTHS
        )
        first = harm_count - width if ascending else 0
        outputs = range(first, first + width)

        def body(r, e):
            for j, total in convolve(coeff, sources, r, e, lambda j: None, outputs):
                conv[0, j - first, r, e], conv[1, j - first, r, e] = total

        tiles(unknowns, elements, body)
        for q in range(width):
            for c in range(2):
                out[c, first + q] = image[c, first + q] + product(stack, conv[c, q])

    by_parity(run)


def resident(*values):
    return [pltpu.with_memory_space_constraint(value, pltpu.VMEM) for value in values]


def stay(*values):
    return [pltpu.with_memory_space_constraint(value, pltpu.HBM) for value in values]


def resident_shape(shape, dtype=F32):
    return pltpu.VMEM(shape, dtype)


def from_partner(value, axis, mask):
    return lax.ppermute(value, axis, [(i, i ^ mask) for i in range(lax.axis_size(axis))])


def shape_like(value):
    return jax.ShapeDtypeStruct(value.shape, value.dtype)


def local(
    response,
    base_coeff,
    volume_mat,
    trace_mats,
    lift_mat,
    round_masks,
    send_elem,
    send_face,
    recv_elem,
):
    harm_count, unknowns, elements = response.shape[1:]
    groups = lax.axis_size("harm")
    skip = [(i, (i + 2) % groups if i % 2 == 0 else (i - 2) % groups) for i in range(groups)]
    near, far = [], []
    whole = response
    face_vars = trace_mats.shape[1]
    slots = send_elem.shape[1]
    piece = pl.pallas_call(
        cut_kernel,
        name="cut",
        compiler_params=KERNEL_MEMORY,
        in_specs=[HBM],
        out_specs=VMEM,
        out_shape=resident_shape((2, WIDTHS[0], unknowns, elements)),
        scratch_shapes=[pltpu.SemaphoreType.DMA],
    )(*stay(response))
    later = len(WIDTHS) - 1
    first, lane_bits, places, response, base_coeff, direct, *pieces = pl.pallas_call(
        trace_kernel,
        name="traces",
        compiler_params=KERNEL_MEMORY,
        in_specs=[HBM] * 7,
        out_specs=[VMEM] * (6 + later),
        out_shape=[
            resident_shape((4 * harm_count, face_vars, 2 * slots)),
            resident_shape((16, 2 * slots), jnp.int32),
            resident_shape((8, 4 * slots), jnp.int32),
            resident_shape(response.shape),
            resident_shape(base_coeff.shape),
            resident_shape((2, 1, unknowns, elements)),
        ]
        + [resident_shape((2, width, unknowns, elements)) for width in WIDTHS[1:]],
        scratch_shapes=[pltpu.VMEM((2 * harm_count * unknowns, 4 * slots), BF16)] * 2
        + [pltpu.SMEM(round_masks.shape, jnp.int32), pltpu.VMEM(trace_mats.shape, F32)]
        + [pltpu.VMEM(send_elem.shape, jnp.int32)] * 3
        + [pltpu.SemaphoreType.DMA((8 + later,))],
    )(*stay(round_masks, response, base_coeff, trace_mats, send_elem, send_face, recv_elem))
    for value in [piece, *pieces]:
        near.append(from_partner(value, "harm", 1))
    relayed = pl.pallas_call(
        relay_kernel,
        name="relay",
        compiler_params=KERNEL_MEMORY,
        in_specs=[VMEM],
        out_specs=VMEM,
        out_shape=resident_shape((2, 1, unknowns, elements)),
    )(*resident(near[-1]))
    for value in [*near[:-1], relayed]:
        far.append(lax.ppermute(value, "harm", skip))
    across = [(i, (i + 1) % groups if i % 2 == 1 else (i - 1) % groups) for i in range(groups)]
    far.append(lax.ppermute(direct, "harm", across))

    small = from_partner(first, "dom", 1)

    def choice(kernel, rows, *values):
        shapes = [resident_shape((n * harm_count, face_vars, 2 * slots)) for n in rows]
        return pl.pallas_call(
            kernel,
            name="choice",
            compiler_params=KERNEL_MEMORY,
            in_specs=[VMEM] * (1 + len(values)),
            out_specs=[VMEM] * len(rows),
            out_shape=shapes,
        )(*resident(lane_bits, *values))

    def stage(value, mask):
        return from_partner(value, "dom", mask)

    part = functools.partial
    kept_x, kept_y = choice(split_kernel, (2, 1), small, first)
    moved_x = stage(kept_x, 2)
    moved_y = stage(kept_y, 12)
    kept_x, rider = choice(part(first_x_kernel, 1), (1, 1), moved_x, kept_x)
    moved_x = stage(kept_x, 4)
    (kept_y,) = choice(part(y_kernel, 3), (1,), moved_y, kept_y)
    moved_y = stage(kept_y, 2)
    (kept_x,) = choice(part(second_x_kernel, 2), (2,), moved_x, kept_x, rider)
    moved_x = stage(kept_x, 12)
    (kept_y,) = choice(part(y_kernel, 1), (1,), moved_y, kept_y)
    moved_y = stage(kept_y, 4)
    (kept,) = choice(part(join_kernel, (3, 2)), (3,), moved_x, kept_x, moved_y, kept_y)
    swapped = stage(kept, 16)

    acc = pl.pallas_call(
        own_kernel,
        name="own",
        compiler_params=KERNEL_MEMORY,
        in_specs=[VMEM] * 2,
        out_specs=VMEM,
        out_shape=resident_shape(response.shape),
    )(*resident(response, base_coeff))

    def near_call(acc, first, chunks):
        return pl.pallas_call(
            lambda *refs: near_kernel(first, *refs),
            name="near",
            compiler_params=KERNEL_MEMORY,
            in_specs=[VMEM] * (2 + len(chunks)),
            out_specs=VMEM,
            out_shape=resident_shape(response.shape),
        )(*resident(base_coeff, acc, *chunks))

    acc = near_call(acc, 0, near[:EARLY])
    acc = near_call(acc, EARLY, near[EARLY:])
    image = pl.pallas_call(
        main_kernel,
        name="main",
        compiler_params=KERNEL_MEMORY,
        in_specs=[VMEM] * (4 + FAR_EARLY),
        out_specs=VMEM,
        out_shape=resident_shape(response.shape),
        scratch_shapes=[pltpu.VMEM(response.shape, F32)],
    )(*resident(base_coeff, response, acc), volume_mat, *resident(*far[:FAR_EARLY]))
    edge_shape = (2, sum(FAR_WIDTHS[FAR_EARLY:]), unknowns, elements)
    image = pl.pallas_call(
        edge_kernel,
        name="edge",
        compiler_params=KERNEL_MEMORY,
        in_specs=[VMEM] * 5,
        out_specs=VMEM,
        out_shape=resident_shape(response.shape),
        input_output_aliases={4: 0},
        scratch_shapes=[pltpu.VMEM(edge_shape, F32)],
    )(*resident(base_coeff), volume_mat, *resident(*far[FAR_EARLY:], image))
    return pl.pallas_call(
        lift_kernel,
        name="lift",
        compiler_params=KERNEL_MEMORY,
        in_specs=[VMEM] * 7,
        out_specs=HBM,
        out_shape=shape_like(whole),
        scratch_shapes=[
            pltpu.VMEM((2 * harm_count * face_vars, elements), F32),
            pltpu.VMEM(response.shape, F32),
            pltpu.SemaphoreType.DMA((harm_count,)),
        ],
    )(
        *resident(image), lift_mat.T, *resident(places, lane_bits, small, swapped, kept),
    )


def solution(mesh):
    in_specs = (
        P(None, "harm", None, "dom"),
        P(None, None, None, "dom"),
        P(),
        P(),
        P(),
        P(),
        P(None, "dom"),
        P(None, "dom"),
        P(None, "dom"),
    )
    out_specs = P(None, "harm", None, "dom")

    return jax.shard_map(local, mesh=mesh, in_specs=in_specs, out_specs=out_specs, check_vma=False)
```
